32 devices in a mesh: energy: 16 (over z, y, x), space: 2 (over core).
Axes of the slice: x: 2, y: 2, z: 4, core: 2. Of those that a mesh axis runs over, the one named last changes fastest.
Arguments:
- lesser: bfloat16 [32, 2, 2, 384, 384], P('energy', 'space'), may hold values from -6 to 6
- coupling: bfloat16 [2, 2, 384, 384], P('space'), may hold values from -0.21875 to 0.21875
- neighbours: int32 [2, 3], P('space'), may hold values from 0 to 1, as said below
- greater: bfloat16 [32, 2, 2, 384, 384], P(None, 'space', None, 'energy'), may hold values from -0.75 to 0.75
- closing: bfloat16 [2, 2, 384, 384], P('space'), may hold values from -0.21875 to 0.21875
Outputs:
- sigma: bfloat16 [32, 2, 2, 384, 384], P('energy', 'space')
The draws below stay inside these ranges and needn't reach their ends.
Inputs may be any that keep to these rules, and one draw needn't show every extreme that they name: `neighbours`: row i names only blocks i - 1, i and i + 1, clipped to 0 .. 1; every row other than the first and the last names both i - 1 and i + 1.
All inputs are finite; a program needn't handle non-finite values.
Results may differ from the reference program's by a relative error of at most 0.007.
Values may be sent and summed in bfloat16 or wider, within the bound.
A program may use at most 64 MiB of HBM per device.

```python
import jax
import jax.numpy as jnp
from jax import lax

ORDER = 384
NE = 32
NB = 2


def draw_neighbours(key, part):
    positions = jnp.arange(NB, dtype=jnp.int32)
    side_sign = 2 * jax.random.randint(jax.random.fold_in(key, 11), (NB,), 0, 2, dtype=jnp.int32) - 1
    middle = positions + jax.random.randint(jax.random.fold_in(key, 12), (NB,), -1, 2, dtype=jnp.int32)
    table = jnp.stack([positions + side_sign, middle, positions - side_sign], axis=1)
    return jnp.clip(table, 0, NB - 1).astype(jnp.int32)


def block_levels(rng, dims, split, smallest, high):
    factor_of = 1.0
    for axis_at, blocks in split:
        draws = jax.random.uniform(jax.random.fold_in(jax.random.fold_in(rng, 6), axis_at), (blocks,), jnp.float32, smallest / len(split), high / len(split))
        factor_of = factor_of * jnp.repeat(jnp.exp(draws), dims[axis_at] // blocks).reshape((-1,) + (1,) * (len(dims) - 1 - axis_at))
    return factor_of


def bell_draw(stream_key, shape, scale, reach, cuts=(), held_as=jnp.bfloat16):
    level = block_levels(stream_key, shape, cuts, -0.22, 0.18) if cuts else 1.0
    entries = jax.random.normal(stream_key, shape, jnp.float32) * scale * level
    return jnp.minimum(jnp.maximum(entries, -reach), reach).astype(held_as)


def setup_inputs(seed: int = 0) -> dict:
    keys = jax.random.split(jax.random.key(seed), 6)
    lesser = bell_draw(keys[0], (NE, NB, 2, ORDER, ORDER), 1.0, 6.0, ((0, 16), (1, 2)))
    coupling = bell_draw(keys[1], (NB, 2, ORDER, ORDER), (2 * ORDER) ** -0.5, 0.21875, ((0, 2),))
    neighbours = draw_neighbours(jax.random.fold_in(keys[5], 71), 0)
    greater = bell_draw(keys[3], (NE, NB, 2, ORDER, ORDER), (2 * NE) ** -0.5, 0.75, ((1, 2), (3, 16)))
    closing = bell_draw(keys[4], (NB, 2, ORDER, ORDER), (2 * ORDER) ** -0.5, 0.21875, ((0, 2),))
    return {"lesser": lesser, "coupling": coupling, "neighbours": neighbours, "greater": greater, "closing": closing}


def round_half(value):
    return lax.optimization_barrier(value.astype(jnp.bfloat16)).astype(jnp.float32)


def left_product(left_real, left_imag, right_real, right_imag):
    def mult(a, b):
        return jnp.einsum('rs,est->ert', a, b, precision=lax.Precision.HIGHEST)
    return mult(left_real, right_real) - mult(left_imag, right_imag), mult(left_real, right_imag) + mult(left_imag, right_real)


def right_adjoint(left_real, left_imag, right_real, right_imag):
    def mult(a, b):
        return jnp.einsum('ers,ts->ert', a, b, precision=lax.Precision.HIGHEST)
    return mult(left_real, right_real) + mult(left_imag, right_imag), mult(left_imag, right_real) - mult(left_real, right_imag)


def reference(lesser, coupling, neighbours, greater, closing):
    def one_block(index):
        slab = lax.dynamic_index_in_dim(lesser, index, 1, False).astype(jnp.float32)
        table_row = lax.dynamic_index_in_dim(neighbours, index, 0, False)
        total_real = jnp.zeros((NE, ORDER, ORDER), jnp.float32)
        total_imag = jnp.zeros((NE, ORDER, ORDER), jnp.float32)
        for term in range(3):
            matrix = lax.dynamic_index_in_dim(coupling, table_row[term], 0, False).astype(jnp.float32)
            part_real, part_imag = left_product(matrix[0], matrix[1], slab[:, 0], slab[:, 1])
            part_real = round_half(part_real)
            part_imag = round_half(part_imag)
            add_real, add_imag = right_adjoint(part_real, part_imag, matrix[0], matrix[1])
            total_real = total_real + add_real
            total_imag = total_imag + add_imag
        screened = lax.dynamic_index_in_dim(greater, index, 1, False).astype(jnp.float32)
        left_complex = total_real + 1j * total_imag
        right_complex = screened[:, 0] + 1j * screened[:, 1]
        folded = jnp.fft.ifft(jnp.fft.fft(left_complex, axis=0) * jnp.fft.fft(right_complex, axis=0), axis=0)
        conv_real = round_half(jnp.real(folded))
        conv_imag = round_half(jnp.imag(folded))
        final = lax.dynamic_index_in_dim(closing, index, 0, False).astype(jnp.float32)
        mid_real, mid_imag = left_product(final[0], final[1], conv_real, conv_imag)
        mid_real = round_half(mid_real)
        mid_imag = round_half(mid_imag)
        out_real, out_imag = right_adjoint(mid_real, mid_imag, final[0], final[1])
        return jnp.stack([out_real, out_imag], axis=1).astype(jnp.bfloat16)

    result = lax.map(one_block, jnp.arange(NB, dtype=jnp.int32))
    return jnp.swapaxes(result, 0, 1)
```

```python
import cmath
import functools
import math

import jax
import jax.numpy as jnp
from jax import lax
from jax.experimental import pallas as pl
from jax.experimental.pallas import tpu as pltpu
from jax.sharding import PartitionSpec as P

F32 = jnp.float32
BF16 = jnp.bfloat16


def times(value, factor):
    re, im = value
    a, b = factor.real, factor.imag
    if abs(b) < 1e-12:
        if abs(a - 1) < 1e-12:
            return value
        if abs(a + 1) < 1e-12:
            return (-re, -im)
        return (re * a, im * a)
    if abs(a) < 1e-12:
        if abs(b - 1) < 1e-12:
            return (-im, re)
        if abs(b + 1) < 1e-12:
            return (im, -re)
        return (im * -b, re * b)
    if abs(a - b) < 1e-12:
        return ((re - im) * a, (re + im) * a)
    if abs(a + b) < 1e-12:
        return ((re + im) * a, (im - re) * a)
    return (re * a - im * b, re * b + im * a)


def dft(values, sign):
    n = len(values)
    if n == 1:
        return values
    even = dft(values[0::2], sign)
    odd = dft(values[1::2], sign)
    out = [None] * n
    for k in range(n // 2):
        er, ei = even[k]
        angle = k * 4 // n if (k * 4) % n == 0 else None
        if angle == 1:
            orr, oi = odd[k]
            if sign < 0:
                out[k] = (er + oi, ei - orr)
                out[k + n // 2] = (er - oi, ei + orr)
            else:
                out[k] = (er - oi, ei + orr)
                out[k + n // 2] = (er + oi, ei - orr)
            continue
        tr, ti = times(odd[k], cmath.exp(sign * 2j * math.pi * k / n))
        out[k] = (er + tr, ei + ti)
        out[k + n // 2] = (er - tr, ei - ti)
    return out


def dot_nn(a, b):
    return lax.dot_general(a, b, (((1,), (0,)), ((), ())), preferred_element_type=F32)


def dot_nt(a, b):
    return lax.dot_general(a, b, (((1,), (1,)), ((), ())), preferred_element_type=F32)


def kernel(
    ne, ns, pts, rows, order,
    nb_ref, lesser, coupling, greater, closing, out,
    vbuf, gbuf, wbuf, nbuf, left, right, acc, abuf,
    psend, precv, ybuf, what, ssend, srecv, sfull, obuf,
    load_sem, vs_sem, vr_sem, ps_sem, pr_sem, ss_sem, sr_sem, out_sem,
):
    me = lax.axis_index("energy")
    here = lax.axis_index("space")
    each = pts // ne
    outer = 4
    inner = pts // outer
    shifts = (1,) if ns == 2 else (1, ns - 1)

    loads = [
        pltpu.make_async_copy(coupling.at[0], vbuf.at[0], load_sem.at[0]),
        pltpu.make_async_copy(lesser.at[:, 0], gbuf, load_sem.at[1]),
        pltpu.make_async_copy(greater.at[:, 0], wbuf, load_sem.at[2]),
        pltpu.make_async_copy(closing.at[0], nbuf, load_sem.at[3]),
    ]
    for load in loads:
        load.start()

    barrier = pltpu.get_barrier_semaphore()
    for k in range(1, ne):
        pl.semaphore_signal(
            barrier, inc=1, device_id={"energy": lax.rem(me + k, ne)},
            device_id_type=pl.DeviceIdType.MESH,
        )
    for shift in shifts:
        pl.semaphore_signal(
            barrier, inc=1, device_id={"space": lax.rem(here + shift, ns)},
            device_id_type=pl.DeviceIdType.MESH,
        )

    def prepare(matrix):
        re = matrix[0]
        im = matrix[1]
        left[0:order, 0:order] = re
        left[0:order, order:] = -im
        left[order:, 0:order] = im
        left[order:, order:] = re
        right[0:order, 0:order] = re
        right[0:order, order:] = im
        right[order:, 0:order] = -im
        right[order:, order:] = re

    def congruence(stacked):
        mid = dot_nn(left[...], stacked).astype(BF16)
        abuf[:, 0:order] = mid[0:order]
        abuf[:, order:] = mid[order:]
        return dot_nt(abuf[...], right[...])

    def weight(block):
        total = jnp.int32(0)
        for term in range(3):
            total = total + jnp.where(nb_ref[0, term] == block, 1, 0)
        return total.astype(F32)

    def energy_slab(e):
        return gbuf[e].reshape(2 * order, order)

    loads[0].wait()
    prepare(vbuf.at[0])
    loads[1].wait()
    own = weight(here)
    acc[0] = congruence(energy_slab(0)) * own

    pl.semaphore_wait(barrier, ne - 1 + len(shifts))
    vcopies = []
    for at, shift in enumerate(shifts):
        copy = pltpu.make_async_remote_copy(
            src_ref=coupling.at[0], dst_ref=vbuf.at[1 + at],
            send_sem=vs_sem.at[at], recv_sem=vr_sem.at[at],
            device_id={"space": lax.rem(here + shift, ns)},
            device_id_type=pl.DeviceIdType.MESH,
        )
        copy.start()
        vcopies.append(copy)
    for e in range(1, each):
        acc[e] = congruence(energy_slab(e)) * own

    pcopies = []
    for at, shift in enumerate(shifts):
        vcopies[at].wait()
        prepare(vbuf.at[1 + at])
        other = weight(lax.rem(here + ns - shift, ns))
        for e in range(each):
            total = acc[e] + congruence(energy_slab(e)) * other
            if at < len(shifts) - 1:
                acc[e] = total
                continue
            for j in range(ne):
                psend[e, j, 0] = total[j * rows:(j + 1) * rows, 0:order].astype(BF16)
                psend[e, j, 1] = total[j * rows:(j + 1) * rows, order:].astype(BF16)
            for k in range(1, ne):
                peer = lax.rem(me + k, ne)
                copy = pltpu.make_async_remote_copy(
                    src_ref=psend.at[e, peer], dst_ref=precv.at[me * each + e],
                    send_sem=ps_sem.at[e, k], recv_sem=pr_sem.at[e, k],
                    device_id={"energy": peer}, device_id_type=pl.DeviceIdType.MESH,
                )
                copy.start()
                pcopies.append(copy)
            precv[me * each + e] = psend[e, me]

    root = lambda power: cmath.exp(-2j * math.pi * power / pts)
    lanes = 128
    chunk = 8 if rows % 8 == 0 else rows

    def outer_forward(source):
        def step(c, carry):
            at = pl.ds(pl.multiple_of(c * lanes, lanes), lanes)
            for n2 in range(inner):
                taken = [
                    (source[inner * n1 + n2, 0, :, at].astype(F32),
                     source[inner * n1 + n2, 1, :, at].astype(F32))
                    for n1 in range(outer)
                ]
                for k1, value in enumerate(dft(taken, -1)):
                    re, im = times(value, root(n2 * k1))
                    ybuf[k1, n2, 0, :, at] = re
                    ybuf[k1, n2, 1, :, at] = im
            return carry

        lax.fori_loop(0, order // lanes, step, 0)

    def over_tiles(body):
        across = order // lanes

        def step(c, carry):
            at = (
                slice(None) if chunk == rows
                else pl.ds(pl.multiple_of((c // across) * chunk, chunk), chunk),
                pl.ds(pl.multiple_of((c % across) * lanes, lanes), lanes),
            )
            body(at)
            return carry

        lax.fori_loop(0, (rows // chunk) * across, step, 0)

    def screened(at):
        for k1 in range(outer):
            taken = [(ybuf[(k1, n2, 0) + at], ybuf[(k1, n2, 1) + at]) for n2 in range(inner)]
            for k2, (re, im) in enumerate(dft(taken, -1)):
                what[(k1, k2, 0) + at] = re * (1.0 / pts)
                what[(k1, k2, 1) + at] = im * (1.0 / pts)

    def middle(at):
        for k1 in range(outer):
            taken = [(ybuf[(k1, n2, 0) + at], ybuf[(k1, n2, 1) + at]) for n2 in range(inner)]
            made = []
            for k2, (re, im) in enumerate(dft(taken, -1)):
                wr = what[(k1, k2, 0) + at]
                wi = what[(k1, k2, 1) + at]
                made.append((re * wr - im * wi, re * wi + im * wr))
            for n2, value in enumerate(dft(made, 1)):
                re, im = times(value, root(-n2 * k1))
                ybuf[(k1, n2, 0) + at] = re
                ybuf[(k1, n2, 1) + at] = im

    def outer_back():
        def step(c, carry):
            at = pl.ds(pl.multiple_of(c * lanes, lanes), lanes)
            for n2 in range(inner):
                taken = [
                    (ybuf[k1, n2, 0, :, at], ybuf[k1, n2, 1, :, at]) for k1 in range(outer)
                ]
                for n1, (re, im) in enumerate(dft(taken, 1)):
                    ssend[inner * n1 + n2, 0, :, at] = re.astype(BF16)
                    ssend[inner * n1 + n2, 1, :, at] = im.astype(BF16)
            return carry

        lax.fori_loop(0, order // lanes, step, 0)

    loads[2].wait()
    outer_forward(wbuf)
    over_tiles(screened)
    loads[3].wait()
    prepare(nbuf)

    for copy in pcopies:
        copy.wait_recv()
    outer_forward(precv)
    over_tiles(middle)
    outer_back()

    scopies = []
    for e in range(each):
        for k in range(1, ne):
            peer = lax.rem(me + k, ne)
            copy = pltpu.make_async_remote_copy(
                src_ref=ssend.at[peer * each + e], dst_ref=srecv.at[e, me],
                send_sem=ss_sem.at[e, k], recv_sem=sr_sem.at[e, k],
                device_id={"energy": peer}, device_id_type=pl.DeviceIdType.MESH,
            )
            copy.start()
            scopies.append(copy)
        srecv[e, me] = ssend[me * each + e]

    for copy in pcopies:
        copy.wait_send()

    stores = []
    for e in range(each):
        for copy in scopies[e * (ne - 1):(e + 1) * (ne - 1)]:
            copy.wait_recv()
        for j in range(ne):
            for part in range(2):
                sfull[part * order + j * rows:part * order + (j + 1) * rows, :] = (
                    srecv[e, j, part].astype(F32)
                )
        result = congruence(sfull[...].astype(BF16)).astype(BF16)
        obuf[e, 0] = result[:, 0:order]
        obuf[e, 1] = result[:, order:]
        store = pltpu.make_async_copy(obuf.at[e], out.at[e, 0], out_sem.at[e])
        store.start()
        stores.append(store)
    for copy in scopies:
        copy.wait_send()
    for store in stores:
        store.wait()


def local(ne, ns, lesser, coupling, neighbours, greater, closing):
    each = lesser.shape[0]
    pts = greater.shape[0]
    rows, order = greater.shape[3], greater.shape[4]
    outer = 4
    cands = 1 if ns == 2 else 2
    anywhere = pl.BlockSpec(memory_space=pl.ANY)
    dma = pltpu.SemaphoreType.DMA
    return pl.pallas_call(
        functools.partial(kernel, ne, ns, pts, rows, order),
        out_shape=jax.ShapeDtypeStruct(lesser.shape, BF16),
        in_specs=[pl.BlockSpec(memory_space=pltpu.SMEM)] + [anywhere] * 4,
        out_specs=anywhere,
        scratch_shapes=[
            pltpu.VMEM((1 + cands, 2, order, order), BF16),
            pltpu.VMEM((each, 2, order, order), BF16),
            pltpu.VMEM((pts, 2, rows, order), BF16),
            pltpu.VMEM((2, order, order), BF16),
            pltpu.VMEM((2 * order, 2 * order), BF16),
            pltpu.VMEM((2 * order, 2 * order), BF16),
            pltpu.VMEM((each, order, 2 * order), F32),
            pltpu.VMEM((order, 2 * order), BF16),
            pltpu.VMEM((each, ne, 2, rows, order), BF16),
            pltpu.VMEM((pts, 2, rows, order), BF16),
            pltpu.VMEM((outer, pts // outer, 2, rows, order), F32),
            pltpu.VMEM((outer, pts // outer, 2, rows, order), F32),
            pltpu.VMEM((pts, 2, rows, order), BF16),
            pltpu.VMEM((each, ne, 2, rows, order), BF16),
            pltpu.VMEM((2 * order, order), F32),
            pltpu.VMEM((each, 2, order, order), BF16),
            dma((4,)), dma((cands,)), dma((cands,)),
            dma((each, ne)), dma((each, ne)), dma((each, ne)), dma((each, ne)),
            dma((each,)),
        ],
        compiler_params=pltpu.CompilerParams(
            collective_id=0, has_side_effects=True, vmem_limit_bytes=60 * 1024 * 1024
        ),
    )(neighbours, lesser, coupling, greater, closing)


def solution(mesh):
    placed = (
        P("energy", "space", None, None, None),
        P("space", None, None, None),
        P("space", None),
        P(None, "space", None, "energy", None),
        P("space", None, None, None),
    )
    return jax.shard_map(
        functools.partial(local, mesh.shape["energy"], mesh.shape["space"]),
        mesh=mesh,
        in_specs=placed,
        out_specs=P("energy", "space", None, None, None),
        check_vma=False,
    )
```

```python
import cmath
import functools
import math

import jax
import jax.numpy as jnp
from jax import lax
from jax.experimental import pallas as pl
from jax.experimental.pallas import tpu as pltpu
from jax.sharding import PartitionSpec as P

F32 = jnp.float32
BF16 = jnp.bfloat16
VMEM_LIMIT = 48 * 1024 * 1024


def times(value, factor):
    re, im = value
    a, b = factor.real, factor.imag
    if abs(b) < 1e-12:
        if abs(a - 1) < 1e-12:
            return value
        if abs(a + 1) < 1e-12:
            return (-re, -im)
        return (re * a, im * a)
    if abs(a) < 1e-12:
        if abs(b - 1) < 1e-12:
            return (-im, re)
        if abs(b + 1) < 1e-12:
            return (im, -re)
        return (im * -b, re * b)
    if abs(a - b) < 1e-12:
        return ((re - im) * a, (re + im) * a)
    if abs(a + b) < 1e-12:
        return ((re + im) * a, (im - re) * a)
    return (re * a - im * b, re * b + im * a)


def dft(values, sign):
    n = len(values)
    if n == 1:
        return values
    even = dft(values[0::2], sign)
    odd = dft(values[1::2], sign)
    out = [None] * n
    for k in range(n // 2):
        er, ei = even[k]
        angle = k * 4 // n if (k * 4) % n == 0 else None
        if angle == 1:
            orr, oi = odd[k]
            if sign < 0:
                out[k] = (er + oi, ei - orr)
                out[k + n // 2] = (er - oi, ei + orr)
            else:
                out[k] = (er - oi, ei + orr)
                out[k + n // 2] = (er + oi, ei - orr)
            continue
        tr, ti = times(odd[k], cmath.exp(sign * 2j * math.pi * k / n))
        out[k] = (er + tr, ei + ti)
        out[k + n // 2] = (er - tr, ei - ti)
    return out


def dot_nn(a, b):
    return lax.dot_general(a, b, (((1,), (0,)), ((), ())), preferred_element_type=F32)


def dot_nt(a, b):
    return lax.dot_general(a, b, (((1,), (1,)), ((), ())), preferred_element_type=F32)


def kernel(
    ne, ns, pts, rows, order, widths,
    nb_ref, lesser, coupling, greater, closing, out,
    vbuf, gbuf, wbuf, nbuf, gemb, acc, abuf, ybuf, what, sfull, semb, obuf,
    psend, precv, ssend, srecv,
    load_sem, vs_sem, vr_sem, ps_sem, pr_sem, ss_sem, sr_sem, out_sem,
):
    me = lax.axis_index("energy")
    here = lax.axis_index("space")
    each = pts // ne
    outer = 4
    inner = pts // outer
    shifts = (1,) if ns == 2 else (1, ns - 1)
    starts = [sum(widths[:c]) for c in range(len(widths))]
    chunks = range(len(widths))

    loads = [
        pltpu.make_async_copy(lesser.at[:, 0], gbuf, load_sem.at[0]),
        pltpu.make_async_copy(coupling.at[0, 0], vbuf.at[0, :, 0:order], load_sem.at[1]),
        pltpu.make_async_copy(coupling.at[0, 1], vbuf.at[0, :, order:], load_sem.at[2]),
        pltpu.make_async_copy(greater.at[:, 0], wbuf, load_sem.at[3]),
        pltpu.make_async_copy(closing.at[0, 0], nbuf.at[:, 0:order], load_sem.at[4]),
        pltpu.make_async_copy(closing.at[0, 1], nbuf.at[:, order:], load_sem.at[5]),
    ]
    for load in loads:
        load.start()

    barrier = pltpu.get_barrier_semaphore()
    for k in range(1, ne):
        pl.semaphore_signal(
            barrier, inc=1, device_id={"energy": lax.rem(me + k, ne)},
            device_id_type=pl.DeviceIdType.MESH,
        )
    for shift in shifts:
        pl.semaphore_signal(
            barrier, inc=1, device_id={"space": lax.rem(here + shift, ns)},
            device_id_type=pl.DeviceIdType.MESH,
        )

    def embed(e):
        re = gbuf[e, 0]
        im = gbuf[e, 1]
        gemb[e, 0:order, 0:order] = re
        gemb[e, 0:order, order:] = im
        gemb[e, order:, 0:order] = -im
        gemb[e, order:, order:] = re

    def place(slot, re, im, start, width):
        at = slice(start, start + width)
        to = slice(order + start, order + start + width)
        abuf[slot, 0:order, at] = re
        abuf[slot, 0:order, to] = im
        abuf[slot, order:, at] = im
        abuf[slot, order:, to] = -re

    def left(slot, e, at):
        mid = dot_nn(vbuf[at], gemb[e]).astype(BF16)
        place(slot, mid[:, 0:order], mid[:, order:], 0, order)

    def weight(block):
        total = jnp.int32(0)
        for term in range(3):
            total = total + jnp.where(nb_ref[0, term] == block, 1, 0)
        return total.astype(F32)

    def own_term(e):
        left(0, e, 0)
        acc[e] = dot_nt(abuf[0], vbuf[0]) * own

    own = weight(here)
    loads[0].wait()
    embed(0)
    loads[1].wait()
    loads[2].wait()
    own_term(0)
    for e in range(1, each):
        embed(e)

    pl.semaphore_wait(barrier, ne - 1 + len(shifts))
    vcopies = []
    for at, shift in enumerate(shifts):
        for part in range(2):
            copy = pltpu.make_async_remote_copy(
                src_ref=coupling.at[0, part],
                dst_ref=vbuf.at[1 + at, :, part * order:(part + 1) * order],
                send_sem=vs_sem.at[at, part], recv_sem=vr_sem.at[at, part],
                device_id={"space": lax.rem(here + shift, ns)},
                device_id_type=pl.DeviceIdType.MESH,
            )
            copy.start()
            vcopies.append(copy)
    for e in range(1, each):
        own_term(e)
    for copy in vcopies:
        copy.wait()
    others = [weight(lax.rem(here + ns - shift, ns)) for shift in shifts]
    for at in range(len(shifts) - 1):
        for e in range(each):
            left(0, e, 1 + at)
            acc[e] = acc[e] + dot_nt(abuf[0], vbuf[1 + at]) * others[at]
    last = len(shifts)

    def last_term(e, c):
        span = slice(starts[c], starts[c] + widths[c])
        total = acc[e, :, span] + dot_nt(abuf[e], vbuf[last, span]) * others[-1]
        for j in range(ne):
            for part in range(2):
                psend[c][e, j, part] = total[
                    part * order + j * rows:part * order + (j + 1) * rows
                ].astype(BF16)

    pcopies = [[] for _ in chunks]

    def send_p(e, c):
        for k in range(1, ne):
            peer = lax.rem(me + k, ne)
            copy = pltpu.make_async_remote_copy(
                src_ref=psend[c].at[e, peer], dst_ref=precv[c].at[me * each + e],
                send_sem=ps_sem.at[c, e, k], recv_sem=pr_sem.at[c, e, k],
                device_id={"energy": peer}, device_id_type=pl.DeviceIdType.MESH,
            )
            copy.start()
            pcopies[c].append(copy)
        precv[c][me * each + e] = psend[c][e, me]

    for c in chunks:
        for e in range(each):
            if c == 0:
                left(e, e, last)
            last_term(e, c)
            send_p(e, c)

    root = lambda power: cmath.exp(-2j * math.pi * power / pts)
    lanes = 128
    chunk = 8 if rows % 8 == 0 else rows

    def lane_tiles(start, width, body):
        def step(c, carry):
            body(
                pl.ds(pl.multiple_of(start + c * lanes, lanes), lanes),
                pl.ds(pl.multiple_of(c * lanes, lanes), lanes),
            )
            return carry

        lax.fori_loop(0, width // lanes, step, 0)

    def outer_forward(source, start, width):
        def body(at, near):
            for n2 in range(inner):
                taken = [
                    (source[inner * n1 + n2, 0, :, near].astype(F32),
                     source[inner * n1 + n2, 1, :, near].astype(F32))
                    for n1 in range(outer)
                ]
                for k1, value in enumerate(dft(taken, -1)):
                    re, im = times(value, root(n2 * k1))
                    ybuf[k1, n2, 0, :, at] = re
                    ybuf[k1, n2, 1, :, at] = im

        lane_tiles(start, width, body)

    def over_tiles(start, width, body):
        across = width // lanes

        def step(c, carry):
            at = (
                slice(None) if chunk == rows
                else pl.ds(pl.multiple_of((c // across) * chunk, chunk), chunk),
                pl.ds(pl.multiple_of(start + (c % across) * lanes, lanes), lanes),
            )
            body(at)
            return carry

        lax.fori_loop(0, (rows // chunk) * across, step, 0)

    def screened(at):
        for k1 in range(outer):
            taken = [(ybuf[(k1, n2, 0) + at], ybuf[(k1, n2, 1) + at]) for n2 in range(inner)]
            for k2, (re, im) in enumerate(dft(taken, -1)):
                what[(k1, k2, 0) + at] = re * (1.0 / pts)
                what[(k1, k2, 1) + at] = im * (1.0 / pts)

    def middle(at):
        for k1 in range(outer):
            taken = [(ybuf[(k1, n2, 0) + at], ybuf[(k1, n2, 1) + at]) for n2 in range(inner)]
            made = []
            for k2, (re, im) in enumerate(dft(taken, -1)):
                wr = what[(k1, k2, 0) + at]
                wi = what[(k1, k2, 1) + at]
                made.append((re * wr - im * wi, re * wi + im * wr))
            for n2, value in enumerate(dft(made, 1)):
                re, im = times(value, root(-n2 * k1))
                ybuf[(k1, n2, 0) + at] = re
                ybuf[(k1, n2, 1) + at] = im

    def outer_back(target, start, width):
        def body(at, near):
            for n2 in range(inner):
                taken = [
                    (ybuf[k1, n2, 0, :, at], ybuf[k1, n2, 1, :, at]) for k1 in range(outer)
                ]
                for n1, (re, im) in enumerate(dft(taken, 1)):
                    target[inner * n1 + n2, 0, :, near] = re.astype(BF16)
                    target[inner * n1 + n2, 1, :, near] = im.astype(BF16)

        lane_tiles(start, width, body)

    loads[3].wait()
    outer_forward(wbuf, 0, order)
    over_tiles(0, order, screened)
    loads[4].wait()
    loads[5].wait()

    scopies = {}
    for c in chunks:
        for copy in pcopies[c]:
            copy.wait_recv()
        outer_forward(precv[c], starts[c], widths[c])
        over_tiles(starts[c], widths[c], middle)
        outer_back(ssend[c], starts[c], widths[c])
        for e in range(each):
            scopies[c, e] = []
            for k in range(1, ne):
                peer = lax.rem(me + k, ne)
                copy = pltpu.make_async_remote_copy(
                    src_ref=ssend[c].at[peer * each + e], dst_ref=srecv[c].at[e, me],
                    send_sem=ss_sem.at[c, e, k], recv_sem=sr_sem.at[c, e, k],
                    device_id={"energy": peer}, device_id_type=pl.DeviceIdType.MESH,
                )
                copy.start()
                scopies[c, e].append(copy)
            srecv[c][e, me] = ssend[c][me * each + e]

    stores = []
    for c in chunks:
        width = widths[c]
        for e in range(each):
            for copy in scopies[c, e]:
                copy.wait_recv()
            for j in range(ne):
                for part in range(2):
                    sfull[part, j * rows:(j + 1) * rows, 0:width] = (
                        srecv[c][e, j, part].astype(F32)
                    )
            re = sfull[0, :, 0:width].astype(BF16)
            im = sfull[1, :, 0:width].astype(BF16)
            semb[0:order, 0:width] = re
            semb[0:order, width:2 * width] = im
            semb[order:, 0:width] = -im
            semb[order:, width:2 * width] = re
            mid = dot_nn(nbuf[...], semb[:, 0:2 * width]).astype(BF16)
            place(e, mid[:, 0:width], mid[:, width:], starts[c], width)
            if c < len(widths) - 1:
                continue
            result = dot_nt(abuf[e], nbuf[...]).astype(BF16)
            obuf[e, 0] = result[0:order]
            obuf[e, 1] = result[order:]
            store = pltpu.make_async_copy(obuf.at[e], out.at[e, 0], out_sem.at[e])
            store.start()
            stores.append(store)
    for c in chunks:
        for copy in pcopies[c]:
            copy.wait_send()
        for e in range(each):
            for copy in scopies[c, e]:
                copy.wait_send()
    for store in stores:
        store.wait()


def local(ne, ns, lesser, coupling, neighbours, greater, closing):
    each = lesser.shape[0]
    pts = greater.shape[0]
    rows, order = greater.shape[3], greater.shape[4]
    outer = 4
    cands = 1 if ns == 2 else 2
    tail = max(1, order // 128 // 3) * 128
    widths = (order - tail, tail)
    resident = pl.BlockSpec(memory_space=pltpu.HBM)
    dma = pltpu.SemaphoreType.DMA
    spread = [pltpu.VMEM((each, ne, 2, rows, width), BF16) for width in widths]
    whole = [pltpu.VMEM((pts, 2, rows, width), BF16) for width in widths]
    counts = dma((len(widths), each, ne))
    return pl.pallas_call(
        functools.partial(kernel, ne, ns, pts, rows, order, widths),
        out_shape=jax.ShapeDtypeStruct(lesser.shape, BF16),
        in_specs=[pl.BlockSpec(memory_space=pltpu.SMEM)] + [resident] * 4,
        out_specs=pl.BlockSpec(memory_space=pl.ANY),
        scratch_shapes=[
            pltpu.VMEM((1 + cands, order, 2 * order), BF16),
            pltpu.VMEM((each, 2, order, order), BF16),
            pltpu.VMEM((pts, 2, rows, order), BF16),
            pltpu.VMEM((order, 2 * order), BF16),
            pltpu.VMEM((each, 2 * order, 2 * order), BF16),
            pltpu.VMEM((each, 2 * order, order), F32),
            pltpu.VMEM((each, 2 * order, 2 * order), BF16),
            pltpu.VMEM((outer, pts // outer, 2, rows, order), F32),
            pltpu.VMEM((outer, pts // outer, 2, rows, order), F32),
            pltpu.VMEM((2, order, widths[0]), F32),
            pltpu.VMEM((2 * order, 2 * widths[0]), BF16),
            pltpu.VMEM((each, 2, order, order), BF16),
            spread, whole, whole, spread,
            dma((6,)), dma((cands, 2)), dma((cands, 2)),
            counts, counts, counts, counts,
            dma((each,)),
        ],
        compiler_params=pltpu.CompilerParams(
            collective_id=0, has_side_effects=True, vmem_limit_bytes=VMEM_LIMIT
        ),
    )(*(
        pltpu.with_memory_space_constraint(x, pltpu.HBM)
        for x in (neighbours, lesser, coupling, greater, closing)
    ))


def solution(mesh):
    placed = (
        P("energy", "space", None, None, None),
        P("space", None, None, None),
        P("space", None),
        P(None, "space", None, "energy", None),
        P("space", None, None, None),
    )
    return jax.shard_map(
        functools.partial(local, mesh.shape["energy"], mesh.shape["space"]),
        mesh=mesh,
        in_specs=placed,
        out_specs=P("energy", "space", None, None, None),
        check_vma=False,
    )
```

```python
import cmath
import functools
import math

import jax
import jax.numpy as jnp
from jax import lax
from jax.experimental import pallas as pl
from jax.experimental.pallas import tpu as pltpu
from jax.sharding import PartitionSpec as P

F32 = jnp.float32
BF16 = jnp.bfloat16
VMEM_LIMIT = 48 * 1024 * 1024


def times(value, factor):
    re, im = value
    a, b = factor.real, factor.imag
    if abs(b) < 1e-12:
        if abs(a - 1) < 1e-12:
            return value
        if abs(a + 1) < 1e-12:
            return (-re, -im)
        return (re * a, im * a)
    if abs(a) < 1e-12:
        if abs(b - 1) < 1e-12:
            return (-im, re)
        if abs(b + 1) < 1e-12:
            return (im, -re)
        return (im * -b, re * b)
    if abs(a - b) < 1e-12:
        return ((re - im) * a, (re + im) * a)
    if abs(a + b) < 1e-12:
        return ((re + im) * a, (im - re) * a)
    return (re * a - im * b, re * b + im * a)


def dft(values, sign):
    n = len(values)
    if n == 1:
        return values
    even = dft(values[0::2], sign)
    odd = dft(values[1::2], sign)
    out = [None] * n
    for k in range(n // 2):
        er, ei = even[k]
        angle = k * 4 // n if (k * 4) % n == 0 else None
        if angle == 1:
            orr, oi = odd[k]
            if sign < 0:
                out[k] = (er + oi, ei - orr)
                out[k + n // 2] = (er - oi, ei + orr)
            else:
                out[k] = (er - oi, ei + orr)
                out[k + n // 2] = (er + oi, ei - orr)
            continue
        tr, ti = times(odd[k], cmath.exp(sign * 2j * math.pi * k / n))
        out[k] = (er + tr, ei + ti)
        out[k + n // 2] = (er - tr, ei - ti)
    return out


def dot_nn(a, b):
    return lax.dot_general(a, b, (((1,), (0,)), ((), ())), preferred_element_type=F32)


def dot_nt(a, b):
    return lax.dot_general(a, b, (((1,), (1,)), ((), ())), preferred_element_type=F32)


def kernel(
    ne, ns, pts, rows, order, widths,
    nb_ref, lesser, coupling, greater, closing, out,
    vbuf, gbuf, wbuf, nbuf, gemb, acc, abuf, ybuf, what, sfull, semb, obuf,
    psend, precv, ssend, srecv,
    load_sem, vs_sem, vr_sem, ps_sem, pr_sem, ss_sem, sr_sem, out_sem,
):
    me = lax.axis_index("energy")
    here = lax.axis_index("space")
    each = pts // ne
    outer = 4
    inner = pts // outer
    shifts = (1,) if ns == 2 else (1, ns - 1)
    half = ne // 2
    side = me // half
    peers = [lax.rem(me + k, ne) for k in range(1, ne)]
    starts = [sum(widths[:c]) for c in range(len(widths))]
    chunks = range(len(widths))

    loads = [
        pltpu.make_async_copy(lesser.at[:, 0], gbuf, load_sem.at[0]),
        pltpu.make_async_copy(coupling.at[0, 0], vbuf.at[0, :, 0:order], load_sem.at[1]),
        pltpu.make_async_copy(coupling.at[0, 1], vbuf.at[0, :, order:], load_sem.at[2]),
        pltpu.make_async_copy(greater.at[:, 0], wbuf, load_sem.at[3]),
        pltpu.make_async_copy(closing.at[0, 0], nbuf.at[:, 0:order], load_sem.at[4]),
        pltpu.make_async_copy(closing.at[0, 1], nbuf.at[:, order:], load_sem.at[5]),
    ]
    for load in loads:
        load.start()

    barrier = pltpu.get_barrier_semaphore()
    for peer in peers:
        pl.semaphore_signal(
            barrier, inc=1, device_id={"energy": peer},
            device_id_type=pl.DeviceIdType.MESH,
        )
    for shift in shifts:
        pl.semaphore_signal(
            barrier, inc=1, device_id={"space": lax.rem(here + shift, ns)},
            device_id_type=pl.DeviceIdType.MESH,
        )

    def embed(e):
        re = gbuf[e, 0]
        im = gbuf[e, 1]
        gemb[e, 0:order, 0:order] = re
        gemb[e, 0:order, order:] = im
        gemb[e, order:, 0:order] = -im
        gemb[e, order:, order:] = re

    def place(slot, re, im, start, width):
        at = slice(start, start + width)
        to = slice(order + start, order + start + width)
        abuf[slot, 0:order, at] = re
        abuf[slot, 0:order, to] = im
        abuf[slot, order:, at] = im
        abuf[slot, order:, to] = -re

    def left(slot, e, at):
        mid = dot_nn(vbuf[at], gemb[e]).astype(BF16)
        place(slot, mid[:, 0:order], mid[:, order:], 0, order)

    def weight(block):
        total = jnp.int32(0)
        for term in range(3):
            total = total + jnp.where(nb_ref[0, term] == block, 1, 0)
        return total.astype(F32)

    def own_term(e):
        left(e, e, 0)
        acc[e] = dot_nt(abuf[e], vbuf[0]) * own

    own = weight(here)
    loads[0].wait()
    embed(0)
    loads[1].wait()
    loads[2].wait()

    pl.semaphore_wait(barrier, ne - 1 + len(shifts))
    vcopies = []
    for at, shift in enumerate(shifts):
        for part in range(2):
            copy = pltpu.make_async_remote_copy(
                src_ref=coupling.at[0, part],
                dst_ref=vbuf.at[1 + at, :, part * order:(part + 1) * order],
                send_sem=vs_sem.at[at, part], recv_sem=vr_sem.at[at, part],
                device_id={"space": lax.rem(here + shift, ns)},
                device_id_type=pl.DeviceIdType.MESH,
            )
            copy.start()
            vcopies.append(copy)
    ahead = 1 if len(shifts) == 1 else each
    for e in range(1, ahead):
        embed(e)
    for e in range(ahead):
        own_term(e)
    for copy in vcopies:
        copy.wait()
    others = [weight(lax.rem(here + ns - shift, ns)) for shift in shifts]
    for at in range(len(shifts) - 1):
        for e in range(each):
            left(0, e, 1 + at)
            acc[e] = acc[e] + dot_nt(abuf[0], vbuf[1 + at]) * others[at]
    last = len(shifts)

    def last_term(e, c):
        span = slice(starts[c], starts[c] + widths[c])
        total = acc[e, :, span] + dot_nt(abuf[e], vbuf[last, span]) * others[-1]
        for j in range(ne):
            for part in range(2):
                psend[c][e, j, part] = total[
                    part * order + j * rows:part * order + (j + 1) * rows
                ].astype(BF16)

    pcopies = [[] for _ in chunks]

    def send_p(e, c):
        for k, peer in enumerate(peers):
            copy = pltpu.make_async_remote_copy(
                src_ref=psend[c].at[e, peer], dst_ref=precv[c].at[me * each + e],
                send_sem=ps_sem.at[c, e, k], recv_sem=pr_sem.at[c, e, k],
                device_id={"energy": peer}, device_id_type=pl.DeviceIdType.MESH,
            )
            copy.start()
            pcopies[c].append(copy)
        precv[c][me * each + e] = psend[c][e, me]

    for c in chunks:
        for e in range(each):
            if c == 0:
                if e >= ahead:
                    embed(e)
                    own_term(e)
                left(e, e, last)
            last_term(e, c)
            send_p(e, c)

    root = lambda power: cmath.exp(-2j * math.pi * power / pts)
    lanes = 128
    chunk = 8 if rows % 8 == 0 else rows

    def lane_tiles(start, width, body):
        def step(c, carry):
            body(
                pl.ds(pl.multiple_of(start + c * lanes, lanes), lanes),
                pl.ds(pl.multiple_of(c * lanes, lanes), lanes),
            )
            return carry

        lax.fori_loop(0, width // lanes, step, 0)

    def outer_forward(source, start, width):
        def body(at, near):
            for n2 in range(inner):
                taken = [
                    (source[inner * n1 + n2, 0, :, near].astype(F32),
                     source[inner * n1 + n2, 1, :, near].astype(F32))
                    for n1 in range(outer)
                ]
                for k1, value in enumerate(dft(taken, -1)):
                    re, im = times(value, root(n2 * k1))
                    ybuf[k1, n2, 0, :, at] = re
                    ybuf[k1, n2, 1, :, at] = im

        lane_tiles(start, width, body)

    def over_tiles(start, width, body):
        across = width // lanes

        def step(c, carry):
            at = (
                slice(None) if chunk == rows
                else pl.ds(pl.multiple_of((c // across) * chunk, chunk), chunk),
                pl.ds(pl.multiple_of(start + (c % across) * lanes, lanes), lanes),
            )
            body(at)
            return carry

        lax.fori_loop(0, (rows // chunk) * across, step, 0)

    def screened(at):
        for k1 in range(outer):
            taken = [(ybuf[(k1, n2, 0) + at], ybuf[(k1, n2, 1) + at]) for n2 in range(inner)]
            for k2, (re, im) in enumerate(dft(taken, -1)):
                what[(k1, k2, 0) + at] = re * (1.0 / pts)
                what[(k1, k2, 1) + at] = im * (1.0 / pts)

    def middle(at):
        for k1 in range(outer):
            taken = [(ybuf[(k1, n2, 0) + at], ybuf[(k1, n2, 1) + at]) for n2 in range(inner)]
            made = []
            for k2, (re, im) in enumerate(dft(taken, -1)):
                wr = what[(k1, k2, 0) + at]
                wi = what[(k1, k2, 1) + at]
                made.append((re * wr - im * wi, re * wi + im * wr))
            for n2, value in enumerate(dft(made, 1)):
                re, im = times(value, root(-n2 * k1))
                ybuf[(k1, n2, 0) + at] = re
                ybuf[(k1, n2, 1) + at] = im

    def outer_back(target, start, width):
        def body(at, near):
            for n2 in range(inner):
                taken = [
                    (ybuf[k1, n2, 0, :, at], ybuf[k1, n2, 1, :, at]) for k1 in range(outer)
                ]
                for n1, (re, im) in enumerate(dft(taken, 1)):
                    target[inner * n1 + n2, 0, :, near] = re.astype(BF16)
                    target[inner * n1 + n2, 1, :, near] = im.astype(BF16)

        lane_tiles(start, width, body)

    loads[3].wait()
    outer_forward(wbuf, 0, order)
    over_tiles(0, order, screened)
    loads[4].wait()
    loads[5].wait()

    scopies = {}
    for c in chunks:
        for copy in pcopies[c]:
            copy.wait_recv()
        outer_forward(precv[c], starts[c], widths[c])
        over_tiles(starts[c], widths[c], middle)
        outer_back(ssend[c], starts[c], widths[c])
        for e in range(each):
            scopies[c, e] = []
            for k, peer in enumerate(peers):
                copy = pltpu.make_async_remote_copy(
                    src_ref=ssend[c].at[peer * each + e], dst_ref=srecv[c].at[e, me],
                    send_sem=ss_sem.at[c, e, k], recv_sem=sr_sem.at[c, e, k],
                    device_id={"energy": peer}, device_id_type=pl.DeviceIdType.MESH,
                )
                copy.start()
                scopies[c, e].append(copy)
            srecv[c][e, me] = ssend[c][me * each + e]

    stores = []
    for c in chunks:
        width = widths[c]
        for e in range(each):
            for copy in scopies[c, e]:
                copy.wait_recv()
            for j in range(ne):
                for part in range(2):
                    sfull[part, j * rows:(j + 1) * rows, 0:width] = (
                        srecv[c][e, j, part].astype(F32)
                    )
            re = sfull[0, :, 0:width].astype(BF16)
            im = sfull[1, :, 0:width].astype(BF16)
            semb[0:order, 0:width] = re
            semb[0:order, width:2 * width] = im
            semb[order:, 0:width] = -im
            semb[order:, width:2 * width] = re
            mid = dot_nn(nbuf[...], semb[:, 0:2 * width]).astype(BF16)
            place(e, mid[:, 0:width], mid[:, width:], starts[c], width)
            span = slice(starts[c], starts[c] + width)
            also = slice(order + starts[c], order + starts[c] + width)
            result = dot_nt(abuf[e, :, span], nbuf[:, span]) + dot_nt(abuf[e, :, also], nbuf[:, also])
            if c > 0:
                result = result + acc[e]
            if c < len(widths) - 1:
                acc[e] = result
                continue
            result = result.astype(BF16)
            obuf[e, 0] = result[0:order]
            obuf[e, 1] = result[order:]
            store = pltpu.make_async_copy(obuf.at[e], out.at[e, 0], out_sem.at[e])
            store.start()
            stores.append(store)
    for c in chunks:
        for copy in pcopies[c]:
            copy.wait_send()
        for e in range(each):
            for copy in scopies[c, e]:
                copy.wait_send()
    for store in stores:
        store.wait()


def local(ne, ns, lesser, coupling, neighbours, greater, closing):
    each = lesser.shape[0]
    pts = greater.shape[0]
    rows, order = greater.shape[3], greater.shape[4]
    outer = 4
    cands = 1 if ns == 2 else 2
    tail = max(1, order // 128 // 3) * 128
    widths = (order - tail, tail)
    resident = pl.BlockSpec(memory_space=pltpu.HBM)
    dma = pltpu.SemaphoreType.DMA
    spread = [pltpu.VMEM((each, ne, 2, rows, width), BF16) for width in widths]
    whole = [pltpu.VMEM((pts, 2, rows, width), BF16) for width in widths]
    counts = dma((len(widths), each, ne))
    return pl.pallas_call(
        functools.partial(kernel, ne, ns, pts, rows, order, widths),
        out_shape=jax.ShapeDtypeStruct(lesser.shape, BF16),
        in_specs=[pl.BlockSpec(memory_space=pltpu.SMEM)] + [resident] * 4,
        out_specs=pl.BlockSpec(memory_space=pl.ANY),
        scratch_shapes=[
            pltpu.VMEM((1 + cands, order, 2 * order), BF16),
            pltpu.VMEM((each, 2, order, order), BF16),
            pltpu.VMEM((pts, 2, rows, order), BF16),
            pltpu.VMEM((order, 2 * order), BF16),
            pltpu.VMEM((each, 2 * order, 2 * order), BF16),
            pltpu.VMEM((each, 2 * order, order), F32),
            pltpu.VMEM((each, 2 * order, 2 * order), BF16),
            pltpu.VMEM((outer, pts // outer, 2, rows, order), F32),
            pltpu.VMEM((outer, pts // outer, 2, rows, order), F32),
            pltpu.VMEM((2, order, widths[0]), F32),
            pltpu.VMEM((2 * order, 2 * widths[0]), BF16),
            pltpu.VMEM((each, 2, order, order), BF16),
            spread, whole, whole, spread,
            dma((6,)), dma((cands, 2)), dma((cands, 2)),
            counts, counts, counts, counts,
            dma((each,)),
        ],
        compiler_params=pltpu.CompilerParams(
            collective_id=0, has_side_effects=True, vmem_limit_bytes=VMEM_LIMIT
        ),
    )(*(
        pltpu.with_memory_space_constraint(x, pltpu.HBM)
        for x in (neighbours, lesser, coupling, greater, closing)
    ))


def solution(mesh):
    placed = (
        P("energy", "space", None, None, None),
        P("space", None, None, None),
        P("space", None),
        P(None, "space", None, "energy", None),
        P("space", None, None, None),
    )
    return jax.shard_map(
        functools.partial(local, mesh.shape["energy"], mesh.shape["space"]),
        mesh=mesh,
        in_specs=placed,
        out_specs=P("energy", "space", None, None, None),
        check_vma=False,
    )
```
